512 devices in a mesh: leaf: 32 (over z, core), front: 16 (over x, y).
Axes of the slice: x: 4, y: 4, z: 16, core: 2. Of those that a mesh axis runs over, the one named last changes fastest.
Arguments:
- subtree_rhs: bfloat16 [524288, 256], P(('leaf', 'front')), may hold values from -6 to 6
- subtree_inverse: bfloat16 [524288, 1024], P(('leaf', 'front')), as said below
- coupling: bfloat16 [16384, 1024], P(('leaf', 'front')), may hold values from -0.1875 to 0.1875
- rhs_top: bfloat16 [4096, 256], P(('leaf', 'front')), may hold values from -6 to 6
- rhs_mid: bfloat16 [8192, 256], P(('leaf', 'front')), may hold values from -6 to 6
- rhs_low: bfloat16 [16384, 256], P(('leaf', 'front')), may hold values from -6 to 6
- inverse_top: bfloat16 [32, 16, 8, 4096], P(None, 'front', None, 'leaf'), as said below
- inverse_mid: bfloat16 [16, 16, 16, 8192], P(None, 'front', None, 'leaf'), as said below
- inverse_low: bfloat16 [8, 16, 32, 16384], P(None, 'front', None, 'leaf'), as said below
- update_mid: bfloat16 [16, 16, 16, 2, 4096], P(None, 'front', None, None, 'leaf'), may hold values from -0.0625 to 0.0625
- update_low: bfloat16 [8, 16, 32, 2, 8192], P(None, 'front', None, None, 'leaf'), may hold values from -0.0625 to 0.0625
- front_rows: int32 [7], replicated, may hold values from 1024 to 4096, as said below
Outputs:
- solution_sub: bfloat16 [524288, 256], P(('leaf', 'front'))
- solution_top: bfloat16 [4096, 256], P(('leaf', 'front'))
- solution_mid: bfloat16 [8192, 256], P(('leaf', 'front'))
- solution_low: bfloat16 [16384, 256], P(('leaf', 'front'))
The draws below stay inside these ranges and needn't reach their ends.
Inputs may be any that keep to these rules, and one draw needn't show every extreme that they name: `front_rows`: live rows of the seven fronts in level order; each is a multiple of 128; the root has all 4096 rows, and at least one lowest front has all 4096 rows. `subtree_inverse`: each block of 1024 rows is a lower-triangular matrix with diagonal entries from 0.6 to 1.4. `inverse_top`: each front's block D is lower triangular with diagonal entries from 0.6 to 1.4. `inverse_mid`: each front's block D is lower triangular with diagonal entries from 0.6 to 1.4. `inverse_low`: each front's block D is lower triangular with diagonal entries from 0.6 to 1.4.
All inputs are finite; a program needn't handle non-finite values.
Results may differ from the reference program's by a relative error of at most 0.025.
Values may be sent and summed in bfloat16 or wider, within the bound.
No kernel may reach another device: no remote copies, remote signals or barrier semaphores. Data moves between devices by JAX's collectives and lax.ppermute only.
A program may use at most 64 MiB of HBM per device.

```python
import math
import jax
import jax.numpy as jnp
from jax import lax

SEP = 4096
RHS = 256
LOC = 1024
TOP_GROUP = 32
MID_GROUP = 16
LOW_GROUP = 8
TOP_PIECE = 8
MID_PIECE = 16
LOW_PIECE = 32
FRONT_WAYS = 16
SUBTREES = 512


def lower_factor(key, rows, order):
    noise_key, diag_key = jax.random.split(key)
    row_pos = (jnp.arange(rows, dtype=jnp.int32) % order)[:, None]
    col_pos = jnp.arange(order, dtype=jnp.int32)[None, :]
    noise = jax.random.normal(noise_key, (rows, order), jnp.float32)
    diagonal = jax.random.uniform(diag_key, (rows, order), jnp.float32, 0.7, 1.3)
    below_diag = noise * (0.5 / math.sqrt(order))
    return jnp.where(col_pos < row_pos, below_diag, jnp.where(col_pos == row_pos, diagonal, 0.0))


def draw_subtree_inverse(key, part):
    keys_all = jax.random.split(key, SUBTREES)

    def one_block(block_key):
        return lower_factor(block_key, LOC, LOC).astype(jnp.bfloat16)
    return lax.map(one_block, keys_all).reshape(SUBTREES * LOC, LOC)


def draw_inverse_top(key, part):
    full_block = lower_factor(key, SEP, SEP)
    return full_block.T.reshape(TOP_GROUP, -1, TOP_PIECE, SEP).astype(jnp.bfloat16)


def draw_inverse_mid(key, part):
    full_block = lower_factor(key, 2 * SEP, SEP)
    return full_block.T.reshape(MID_GROUP, -1, MID_PIECE, 2 * SEP).astype(jnp.bfloat16)


def draw_inverse_low(key, part):
    full_block = lower_factor(key, 4 * SEP, SEP)
    return full_block.T.reshape(LOW_GROUP, -1, LOW_PIECE, 4 * SEP).astype(jnp.bfloat16)


def draw_front_rows(key, part):
    size_key, full_key = jax.random.split(key)
    lowest = max(1, SEP // 512)
    blocks = jax.random.randint(size_key, (7,), lowest, SEP // 128 + 1, dtype=jnp.int32)
    full_at = jax.random.randint(full_key, (), 3, 7, dtype=jnp.int32)
    positions = jnp.arange(7, dtype=jnp.int32)
    blocks = jnp.where((positions == full_at) | (positions == 0), SEP // 128, blocks)
    return (blocks * 128).astype(jnp.int32)


def block_levels(own_key, extent, shards, least, top_value):
    loudness, own = 1.0, jax.random.fold_in(own_key, 6)
    for position, blocks in shards:
        draws = jnp.exp(jax.random.uniform(jax.random.fold_in(own, position), (blocks,), jnp.float32, least / len(shards), top_value / len(shards)))
        loudness = loudness * jnp.repeat(draws, extent[position] // blocks).reshape([-1 if axis == position else 1 for axis in range(len(extent))])
    return loudness


def scatter_about(key, extent, deviation, most, cuts=(), held_as=jnp.bfloat16):
    gain = block_levels(key, extent, cuts, -0.22, 0.18) if cuts else 1.0
    entries = jax.random.normal(key, extent, jnp.float32) * deviation * gain
    return jnp.minimum(jnp.maximum(entries, -most), most).astype(held_as)


def setup_inputs(seed: int = 0) -> dict:
    splits = jax.random.split(jax.random.key(seed), 13)
    return {
        "subtree_rhs": scatter_about(splits[0], (SUBTREES * LOC, RHS), 1.0, 6.0, ((0, 512),)),
        "subtree_inverse": draw_subtree_inverse(jax.random.fold_in(splits[12], 71), 0),
        "coupling": scatter_about(splits[2], (4 * SEP, LOC), LOC ** -0.5, 0.1875, ((0, 512),)),
        "rhs_top": scatter_about(splits[3], (SEP, RHS), 1.0, 6.0, ((0, 512),)),
        "rhs_mid": scatter_about(splits[4], (2 * SEP, RHS), 1.0, 6.0, ((0, 512),)),
        "rhs_low": scatter_about(splits[5], (4 * SEP, RHS), 1.0, 6.0, ((0, 512),)),
        "inverse_top": draw_inverse_top(jax.random.fold_in(splits[12], 71), 0),
        "inverse_mid": draw_inverse_mid(jax.random.fold_in(splits[12], 71), 0),
        "inverse_low": draw_inverse_low(jax.random.fold_in(splits[12], 71), 0),
        "update_mid": scatter_about(splits[9], (MID_GROUP, FRONT_WAYS, MID_PIECE, 2, SEP), (2 * SEP) ** -0.5, 0.0625, ((1, 16), (4, 32))),
        "update_low": scatter_about(splits[10], (LOW_GROUP, FRONT_WAYS, LOW_PIECE, 2, 2 * SEP), (2 * SEP) ** -0.5, 0.0625, ((1, 16), (4, 32))),
        "front_rows": draw_front_rows(jax.random.fold_in(splits[12], 71), 0),
    }


def unpack_inverse(stored, front_count):
    flattened = stored.reshape(SEP, front_count * SEP)
    return flattened.T.reshape(front_count, SEP, SEP)


def unpack_update(stored, front_count, groups):
    half_rows = SEP // (2 * groups)
    flattened = stored.reshape(SEP, 2, front_count, groups, half_rows)
    return jnp.transpose(flattened, (2, 1, 3, 4, 0)).reshape(front_count, SEP, SEP)


def level_mask(front_rows, heap_start, front_count):
    row_ids = jnp.arange(SEP, dtype=jnp.int32)
    live_rows = front_rows[heap_start:heap_start + front_count].astype(jnp.int32)
    return (row_ids[None, :] < live_rows[:, None])[:, :, None]


def apply_blocks(blocks, right_side, row_mask, transpose):
    results = []
    for front_pos in range(blocks.shape[0]):
        matrix = blocks[front_pos].T if transpose else blocks[front_pos]
        results.append(jnp.dot(matrix, right_side[front_pos], preferred_element_type=jnp.float32))
    return jnp.where(row_mask, jnp.stack(results), 0.0).astype(jnp.bfloat16)


def lift_rows(updates, solved, parent_rhs, row_mask):
    parents = parent_rhs.shape[0] // SEP
    right_side = parent_rhs.astype(jnp.float32).reshape(parents, SEP, RHS)
    terms = []
    for parent_pos in range(parents):
        running = right_side[parent_pos]
        for child_pos in (2 * parent_pos, 2 * parent_pos + 1):
            running = running - jnp.dot(updates[child_pos], solved[child_pos], preferred_element_type=jnp.float32)
        terms.append(running)
    return jnp.where(row_mask, jnp.stack(terms), 0.0).astype(jnp.bfloat16)


def lower_residual(updates, forward, parent_solution, row_mask):
    terms = []
    for child_pos in range(updates.shape[0]):
        moved = jnp.dot(updates[child_pos].T, parent_solution[child_pos // 2], preferred_element_type=jnp.float32)
        terms.append(forward[child_pos].astype(jnp.float32) - moved)
    return jnp.where(row_mask, jnp.stack(terms), 0.0).astype(jnp.bfloat16)


def reference(subtree_rhs, subtree_inverse, coupling, rhs_top, rhs_mid, rhs_low, inverse_top, inverse_mid, inverse_low, update_mid, update_low, front_rows):
    factor_blocks = subtree_inverse.reshape(SUBTREES, LOC, LOC)
    rhs_blocks = subtree_rhs.reshape(SUBTREES, LOC, RHS)
    coupling_blocks = coupling.reshape(SUBTREES, LOW_PIECE, LOC)

    def subtree_forward(inputs):
        factor, right_side = inputs
        return jnp.dot(factor, right_side, preferred_element_type=jnp.float32).astype(jnp.bfloat16)

    below_solved = lax.map(subtree_forward, (factor_blocks, rhs_blocks))

    def push_rows(inputs):
        link_block, solved = inputs
        return jnp.dot(link_block, solved, preferred_element_type=jnp.float32)

    pushed = lax.map(push_rows, (coupling_blocks, below_solved)).reshape(4, SEP, RHS)

    mask_top = level_mask(front_rows, 0, 1)
    mask_mid = level_mask(front_rows, 1, 2)
    mask_low = level_mask(front_rows, 3, 4)
    blocks_top = unpack_inverse(inverse_top, 1)
    blocks_mid = unpack_inverse(inverse_mid, 2)
    blocks_low = unpack_inverse(inverse_low, 4)
    links_mid = unpack_update(update_mid, 2, MID_GROUP)
    links_low = unpack_update(update_low, 4, LOW_GROUP)

    right_low = jnp.where(mask_low, rhs_low.astype(jnp.float32).reshape(4, SEP, RHS) - pushed, 0.0).astype(jnp.bfloat16)
    forward_low = apply_blocks(blocks_low, right_low, mask_low, False)
    right_mid = lift_rows(links_low, forward_low, rhs_mid, mask_mid)
    forward_mid = apply_blocks(blocks_mid, right_mid, mask_mid, False)
    right_top = lift_rows(links_mid, forward_mid, rhs_top, mask_top)
    forward_top = apply_blocks(blocks_top, right_top, mask_top, False)

    solution_top = apply_blocks(blocks_top, forward_top, mask_top, True)
    residual_mid = lower_residual(links_mid, forward_mid, solution_top, mask_mid)
    solution_mid = apply_blocks(blocks_mid, residual_mid, mask_mid, True)
    residual_low = lower_residual(links_low, forward_low, solution_mid, mask_low)
    solution_low = apply_blocks(blocks_low, residual_low, mask_low, True)

    low_blocks = solution_low.reshape(SUBTREES, LOW_PIECE, RHS)

    def subtree_backward(inputs):
        factor, link_block, solved, low_rows = inputs
        moved = jnp.dot(link_block.T, low_rows, preferred_element_type=jnp.float32)
        shifted = (solved.astype(jnp.float32) - moved).astype(jnp.bfloat16)
        return jnp.dot(factor.T, shifted, preferred_element_type=jnp.float32).astype(jnp.bfloat16)

    solution_sub = lax.map(subtree_backward, (factor_blocks, coupling_blocks, below_solved, low_blocks))
    return (solution_sub.reshape(SUBTREES * LOC, RHS), solution_top.reshape(SEP, RHS), solution_mid.reshape(2 * SEP, RHS), solution_low.reshape(4 * SEP, RHS))
```

```python
import jax
import jax.numpy as jnp
from jax import lax
from jax.sharding import Mesh, PartitionSpec as P

FRONT = ("x", "y")
LEAF = ("mid", "low", "z", "core")
GROUP_AXES = {8: ("z", "core"), 16: ("low", "z", "core"), 32: ("mid", "low", "z", "core")}
SIBLING_AXIS = {8: "low", 16: "mid"}


def swap(array, axis):
    return lax.ppermute(array, axis, [(0, 1), (1, 0)])


def gather(block, axes):
    ways = lax.axis_size(axes)
    sent = jnp.broadcast_to(block[None], (ways,) + block.shape)
    got = lax.all_to_all(sent, axes, 0, 0, tiled=True)
    return got.reshape(ways * block.shape[0], block.shape[1])


def reduce_rows(partial_value, axes):
    ways = lax.axis_size(axes)
    sent = partial_value.astype(jnp.bfloat16).reshape(ways, -1, partial_value.shape[-1])
    got = lax.all_to_all(sent, axes, 0, 0, tiled=True)
    return jnp.sum(got.astype(jnp.float32), axis=0)


def live_mask(front_rows, heap_start, groups, pieces):
    leaf_pos = lax.axis_index(LEAF)
    front_pos = lax.axis_index(FRONT)
    member = leaf_pos % groups
    node_pos = leaf_pos // groups
    lookup = jnp.arange(front_rows.shape[0], dtype=jnp.int32)
    live_rows = jnp.sum(jnp.where(lookup == heap_start + node_pos, front_rows, 0))
    row_offset = (member * lax.axis_size(FRONT) + front_pos) * pieces
    row_ids = row_offset + jnp.arange(pieces, dtype=jnp.int32)
    return (row_ids < live_rows)[:, None]


def forward_front(right_block, inverse, row_mask):
    groups, _, pieces, rows = inverse.shape
    local_inverse = inverse.reshape(groups * pieces, rows)
    columns = gather(right_block, GROUP_AXES[groups])
    summed = reduce_rows(
        lax.dot_general(
            local_inverse, columns, (((0,), (0,)), ((), ())), preferred_element_type=jnp.float32
        ),
        FRONT,
    )
    return jnp.where(row_mask, summed, 0.0).astype(jnp.bfloat16)


def forward_update(child_solved, update, parent_rhs, parent_mask):
    groups, _, pieces, _, half_rows = update.shape
    local_update = update.reshape(groups * pieces, 2 * half_rows)
    columns = gather(child_solved, GROUP_AXES[groups])
    products = lax.dot_general(
        local_update, columns, (((0,), (0,)), ((), ())), preferred_element_type=jnp.float32
    ).reshape(2, lax.axis_size(FRONT), -1, columns.shape[1])
    sent = products.astype(jnp.bfloat16).transpose(1, 0, 2, 3)
    got = lax.all_to_all(sent, FRONT, 0, 0, tiled=True)
    sums = jnp.sum(got.astype(jnp.float32), axis=0)
    axis = SIBLING_AXIS[groups]
    parity = lax.axis_index(axis)
    kept = jnp.where(parity == 0, sums[0], sums[1])
    other = jnp.where(parity == 0, sums[1], sums[0])
    total = kept + swap(other.astype(jnp.bfloat16), axis).astype(jnp.float32)
    return jnp.where(parent_mask, parent_rhs.astype(jnp.float32) - total, 0.0).astype(jnp.bfloat16)


def backward_front(solved_block, inverse, row_mask):
    groups, _, pieces, rows = inverse.shape
    local_inverse = inverse.reshape(groups * pieces, rows)
    partial_value = jnp.dot(
        local_inverse, gather(solved_block, FRONT), preferred_element_type=jnp.float32
    )
    summed = reduce_rows(partial_value, GROUP_AXES[groups])
    return jnp.where(row_mask, summed, 0.0).astype(jnp.bfloat16)


def backward_update(child_forward, update, parent_solution, row_mask):
    groups, _, pieces, _, half_rows = update.shape
    local_update = update.reshape(groups * pieces, 2 * half_rows)
    axis = SIBLING_AXIS[groups]
    parity = lax.axis_index(axis)
    sibling = swap(parent_solution, axis)
    pair = jnp.stack(
        [
            jnp.where(parity == 0, parent_solution, sibling),
            jnp.where(parity == 0, sibling, parent_solution),
        ]
    )
    ways = lax.axis_size(FRONT)
    sent = jnp.broadcast_to(pair[None], (ways,) + pair.shape)
    got = lax.all_to_all(sent, FRONT, 0, 0, tiled=True)
    rows = got.transpose(1, 0, 2, 3).reshape(2 * half_rows, -1)
    partial_value = jnp.dot(local_update, rows, preferred_element_type=jnp.float32)
    summed = reduce_rows(partial_value, GROUP_AXES[groups])
    return jnp.where(row_mask, child_forward.astype(jnp.float32) - summed, 0.0).astype(jnp.bfloat16)


def shards(
    subtree_rhs,
    subtree_inverse,
    coupling,
    rhs_top,
    rhs_mid,
    rhs_low,
    inverse_top,
    inverse_mid,
    inverse_low,
    update_mid,
    update_low,
    front_rows,
):
    below_solved = jnp.dot(subtree_inverse, subtree_rhs, preferred_element_type=jnp.float32).astype(
        jnp.bfloat16
    )
    mask_top = live_mask(front_rows, 0, inverse_top.shape[0], rhs_top.shape[0])
    mask_mid = live_mask(front_rows, 1, inverse_mid.shape[0], rhs_mid.shape[0])
    mask_low = live_mask(front_rows, 3, inverse_low.shape[0], rhs_low.shape[0])
    pushed = jnp.dot(coupling, below_solved, preferred_element_type=jnp.float32)
    right_low = jnp.where(mask_low, rhs_low.astype(jnp.float32) - pushed, 0.0).astype(jnp.bfloat16)
    forward_low = forward_front(right_low, inverse_low, mask_low)
    right_mid = forward_update(forward_low, update_low, rhs_mid, mask_mid)
    forward_mid = forward_front(right_mid, inverse_mid, mask_mid)
    right_top = forward_update(forward_mid, update_mid, rhs_top, mask_top)
    forward_top = forward_front(right_top, inverse_top, mask_top)
    solution_top = backward_front(forward_top, inverse_top, mask_top)
    residual_mid = backward_update(forward_mid, update_mid, solution_top, mask_mid)
    solution_mid = backward_front(residual_mid, inverse_mid, mask_mid)
    residual_low = backward_update(forward_low, update_low, solution_mid, mask_low)
    solution_low = backward_front(residual_low, inverse_low, mask_low)
    moved = lax.dot_general(
        coupling, solution_low, (((0,), (0,)), ((), ())), preferred_element_type=jnp.float32
    )
    shifted = (below_solved.astype(jnp.float32) - moved).astype(jnp.bfloat16)
    solution_sub = lax.dot_general(
        subtree_inverse, shifted, (((0,), (0,)), ((), ())), preferred_element_type=jnp.float32
    ).astype(jnp.bfloat16)
    return (solution_sub, solution_top, solution_mid, solution_low)


def solution(mesh):
    fine = Mesh(mesh.devices.reshape(2, 2, 4, 2, 4, 4), LEAF + FRONT)
    rows = P(LEAF + FRONT, None)
    placed = (
        rows,
        rows,
        rows,
        rows,
        rows,
        rows,
        P(None, FRONT, None, LEAF),
        P(None, FRONT, None, LEAF),
        P(None, FRONT, None, LEAF),
        P(None, FRONT, None, None, LEAF),
        P(None, FRONT, None, None, LEAF),
        P(),
    )
    return jax.shard_map(
        shards, mesh=fine, in_specs=placed, out_specs=(rows, rows, rows, rows), check_vma=False
    )
```

```python
import jax
import jax.numpy as jnp
from jax import lax
from jax.experimental import pallas as pl
from jax.experimental.pallas import tpu as pltpu
from jax.sharding import Mesh, PartitionSpec as P

FRONT = ("x", "y")
LEAF = ("mid", "low", "z", "core")
BLOCK = ("z", "core")
WAYS = 16
MEMBERS = 8
SLICE = 32
ROWS = 32
WIDTH = MEMBERS * SLICE
SMALL = (ROWS, WIDTH)
SENT = (WAYS, ROWS, WIDTH)
FRONT_AT, MID_AT, CORE_AT = 3, 4, 5
F32 = jnp.float32
BF16 = jnp.bfloat16


def swap(array, axis):
    return lax.ppermute(array, axis, [(0, 1), (1, 0)])


def exchange(blocks, axes):
    return lax.all_to_all(blocks, axes, 0, 0, tiled=True)


def gather(block, axes):
    ways = lax.axis_size(axes)
    return exchange(jnp.broadcast_to(block[None], (ways,) + block.shape), axes)


def after(array, chain):
    return array + jnp.minimum(jnp.abs(chain[:1, :1]), 0.0).astype(array.dtype)


def in_order(position, own, other, axis):
    return jnp.where(
        position == 0,
        jnp.concatenate([own, other], axis=axis),
        jnp.concatenate([other, own], axis=axis),
    )


def product_rows(gathered, matrix, piece, out_piece):
    columns = gathered.reshape(MEMBERS, ROWS // piece, piece, WIDTH)
    columns = columns.transpose(1, 0, 2, 3).reshape(MEMBERS * ROWS, WIDTH)
    product = lax.dot_general(
        matrix, columns, (((0,), (0,)), ((), ())), preferred_element_type=F32
    ).astype(BF16)
    product = product.reshape(ROWS // out_piece, WAYS, out_piece, WIDTH).transpose(1, 0, 2, 3)
    return jnp.sum(exchange(product.reshape(SENT), FRONT).astype(F32), axis=0)


def lane_group(rows):
    return lax.broadcasted_iota(jnp.int32, (rows, WIDTH), 1) // SLICE


def packed_mask(table_ref, level, piece):
    row = lax.broadcasted_iota(jnp.int32, SMALL, 0)
    member = row // piece * MEMBERS + lane_group(ROWS)
    index = (member * WAYS + table_ref[FRONT_AT]) * piece + row % piece
    return index < table_ref[level]


def source_rows(recv_ref, piece):
    parts = []
    for o in range(ROWS // piece):
        rows = recv_ref[:, o * piece : (o + 1) * piece, :].astype(F32)
        parts.append(rows.reshape(WAYS * piece, WIDTH))
    return jnp.concatenate(parts, axis=0).astype(BF16)


def apply_transposed(weights_ref, recv_ref, row_piece, piece):
    source = source_rows(recv_ref, row_piece)
    group = lane_group(WIDTH)
    total = jnp.zeros((WIDTH, WIDTH), F32)
    for m in range(MEMBERS):
        term = jnp.dot(weights_ref[m], source, preferred_element_type=F32)
        total = jnp.where(group == m, term, total)
    for step in (4 * SLICE, 2 * SLICE, SLICE):
        total = total + pltpu.roll(total, step, 1)
    group = lane_group(piece)
    packed = []
    for o in range(ROWS // piece):
        rows = jnp.zeros((piece, WIDTH), F32)
        for m in range(MEMBERS):
            start = (o * MEMBERS + m) * piece
            rows = jnp.where(group == m, total[start : start + piece], rows)
        packed.append(rows)
    return jnp.concatenate(packed, axis=0)


def whole(shape):
    return pl.BlockSpec(shape, lambda i: (0,) * len(shape))


def call(body, table, operands, specs, shapes):
    return pl.pallas_call(
        body,
        grid=(1,),
        in_specs=[pl.BlockSpec(memory_space=pltpu.SMEM)] + specs,
        out_specs=[whole(shape) for shape in shapes],
        out_shape=[jax.ShapeDtypeStruct(shape, BF16) for shape in shapes],
        compiler_params=pltpu.CompilerParams(vmem_limit_bytes=32 << 20),
    )(table, *operands)


def weight_spec(part):
    return pl.BlockSpec((MEMBERS, WIDTH, 2 * WIDTH), lambda i: (0, 0, part))


def backward_solve(table, level, recv, weights, piece):
    def body(table_ref, recv_ref, weights_ref, solved_ref, send_ref):
        value = apply_transposed(weights_ref, recv_ref, piece, piece)
        solved = jnp.where(packed_mask(table_ref, level, piece), value, 0.0).astype(BF16)
        solved_ref[...] = solved
        send_ref[...] = jnp.broadcast_to(solved[None], SENT)

    return call(body, table, (recv, weights), [whole(SENT), weight_spec(0)], [SMALL, SENT])


def backward_residual(table, level, recv, forward, weights, row_piece, piece):
    def body(table_ref, recv_ref, forward_ref, weights_ref, send_ref):
        value = forward_ref[...].astype(F32)
        value = value - apply_transposed(weights_ref, recv_ref, row_piece, piece)
        residual = jnp.where(packed_mask(table_ref, level, piece), value, 0.0).astype(BF16)
        send_ref[...] = jnp.broadcast_to(residual[None], SENT)

    return call(
        body,
        table,
        (recv, forward, weights),
        [whole(SENT), whole(SMALL), weight_spec(1)],
        [SENT],
    )[0]


def order_shares(table, shares, chain):
    def body(table_ref, shares_ref, chain_ref, middle_ref, matrix_ref, update_ref, root_ref):
        core = table_ref[CORE_AT]
        for o in range(2):
            block = shares_ref[table_ref[MID_AT] * 4 + o * 2 + core, :, :WIDTH]
            matrix_ref[:, o * WIDTH : (o + 1) * WIDTH] = block
            middle_ref[:, o * WIDTH : (o + 1) * WIDTH] = block
            for h in range(2):
                block = shares_ref[table_ref[MID_AT] * 4 + o * 2 + core, :, WIDTH + h * 128 : WIDTH + h * 128 + 128]
                start = (h * 2 + o) * 128
                update_ref[:, start : start + 128] = block
                middle_ref[:, 2 * WIDTH + start : 2 * WIDTH + start + 128] = block
        for o in range(4):
            root_ref[:, o * 128 : o * 128 + 128] = shares_ref[o * 2 + core, :, 2 * WIDTH :]

    pair = (WIDTH, 2 * WIDTH)
    return call(
        body,
        table,
        (shares, chain),
        [whole(shares.shape), pl.BlockSpec(memory_space=pl.ANY)],
        [(WIDTH, 4 * WIDTH), pair, pair, pair],
    )


SPLIT = (MEMBERS, ROWS + 8, WIDTH)


def root_transposed(table, recv, matrix, kept, piece):
    def body(table_ref, recv_ref, matrix_ref, kept_ref, send_ref):
        product = jnp.dot(
            matrix_ref[...], source_rows(recv_ref, piece), preferred_element_type=F32
        )
        kept_rows = kept_ref[...].astype(F32)
        turned = [product] + [pltpu.roll(product, SLICE * d, 1) for d in range(1, MEMBERS)]
        kept_turned = [kept_rows] + [pltpu.roll(kept_rows, SLICE * d, 1) for d in range(1, MEMBERS)]
        group = lane_group(8)
        for target in range(MEMBERS):
            blocks = []
            for o in range(ROWS // piece):
                rows = jnp.zeros((piece, WIDTH), F32)
                for m in range(MEMBERS):
                    start = (o * MEMBERS + m) * piece
                    moved = turned[(m - target) % MEMBERS][start : start + piece]
                    rows = jnp.where(group == m, moved, rows)
                blocks.append(rows)
            rows = jnp.zeros((8, WIDTH), F32)
            for q in range(8):
                moved = kept_turned[(q - target) % MEMBERS][q * 8 : q * 8 + 8]
                rows = jnp.where(group == q, moved, rows)
            blocks.append(rows)
            send_ref[target] = jnp.concatenate(blocks, axis=0).astype(BF16)

    return call(
        body,
        table,
        (recv, matrix, kept),
        [whole(SENT), whole((WIDTH, 2 * WIDTH)), whole((2 * ROWS, WIDTH))],
        [SPLIT],
    )[0]


def root_collect(table, level, recv, piece):
    def body(table_ref, recv_ref, solved_ref, mid_ref, low_ref, send_ref):
        blocks = [recv_ref[m].astype(F32) for m in range(MEMBERS)]
        total = blocks[0][:ROWS]
        for m in range(1, MEMBERS):
            total = total + blocks[m][:ROWS]
        solved = jnp.where(packed_mask(table_ref, level, piece), total, 0.0).astype(BF16)
        solved_ref[...] = solved
        send_ref[...] = jnp.broadcast_to(solved[None], SENT)
        group = lane_group(8)
        kept = []
        for q in range(8):
            rows = jnp.zeros((8, WIDTH), F32)
            for m in range(MEMBERS):
                moved = blocks[m][ROWS:]
                shift = (m - q) % MEMBERS
                if shift:
                    moved = pltpu.roll(moved, SLICE * shift, 1)
                rows = jnp.where(group == m, moved, rows)
            kept.append(rows)
        mid_ref[...] = jnp.concatenate(kept[:4], axis=0).astype(BF16)
        low_ref[...] = jnp.concatenate(kept[4:], axis=0).astype(BF16)

    return call(body, table, (recv,), [whole(SPLIT)], [SMALL, SMALL, SMALL, SENT])


def from_slices(rows):
    count = rows.shape[0]
    sent = rows.reshape(count, MEMBERS, SLICE).transpose(1, 0, 2)
    return exchange(sent, BLOCK).transpose(1, 0, 2).reshape(count, WIDTH)


def shards(
    subtree_rhs,
    subtree_inverse,
    coupling,
    rhs_top,
    rhs_mid,
    rhs_low,
    inverse_top,
    inverse_mid,
    inverse_low,
    update_mid,
    update_low,
    front_rows,
):
    mid_pos = lax.axis_index("mid")
    low_pos = lax.axis_index("low")
    front_pos = lax.axis_index(FRONT)
    member = lax.axis_index(BLOCK)
    piece_top, piece_mid, piece_low = rhs_top.shape[0], rhs_mid.shape[0], rhs_low.shape[0]
    low_matrix = inverse_low.reshape(WIDTH, -1)
    low_update = update_low.reshape(WIDTH, -1)

    lookup = jnp.arange(front_rows.shape[0], dtype=jnp.int32)

    def live(index):
        return jnp.sum(jnp.where(lookup == index, front_rows, 0))

    def row_mask(live_rows, piece):
        row = jnp.arange(ROWS, dtype=jnp.int32)
        place = (row // piece * MEMBERS + member) * WAYS + front_pos
        return (place * piece + row % piece < live_rows)[:, None]

    live_top, live_mid, live_low = live(0), live(1 + mid_pos), live(3 + mid_pos * 2 + low_pos)
    table = jnp.stack(
        [live_top, live_mid, live_low, front_pos, mid_pos, lax.axis_index("core")]
    ).astype(jnp.int32)
    mask_top = row_mask(live_top, piece_top)
    mask_mid = row_mask(live_mid, piece_mid)
    mask_low = row_mask(live_low, piece_low)

    def rounded(mask, value):
        return jnp.where(mask, value, 0.0).astype(BF16)

    below_solved = jnp.dot(subtree_inverse, subtree_rhs, preferred_element_type=F32).astype(BF16)
    pushed = jnp.dot(coupling, below_solved, preferred_element_type=F32)
    right_low = rounded(mask_low, rhs_low.astype(F32) - pushed)
    columns = gather(right_low, BLOCK)
    own = jnp.concatenate(
        [
            inverse_mid.reshape(WIDTH, -1),
            update_mid.reshape(WIDTH, -1),
            inverse_top.reshape(WIDTH, -1),
        ],
        axis=1,
    )
    shares = lax.all_gather(own, ("mid", "low", "core"), axis=0, tiled=False)
    forward_low = rounded(mask_low, product_rows(columns, low_matrix, piece_low, piece_low))

    lifted = product_rows(gather(forward_low, BLOCK), low_update, piece_low, piece_mid)
    half = jnp.arange(2, dtype=jnp.int32)[:, None, None]
    share = jnp.where(half == low_pos, rhs_mid.astype(F32)[None], 0.0)
    share = (share.reshape(SMALL) - lifted).astype(BF16)
    shared = swap(jnp.concatenate([share, rhs_top], axis=0), "low")
    right_mid = rounded(mask_mid, share.astype(F32) + shared[:ROWS].astype(F32))
    rhs_pair = in_order(low_pos, rhs_top, shared[ROWS:], 0)

    columns = gather(right_mid, BLOCK)
    middle, mid_matrix, mid_update, top_matrix = order_shares(table, shares, right_mid)
    middle = lax.all_gather(middle, BLOCK, axis=0, tiled=False)
    forward_mid = rounded(mask_mid, product_rows(columns, mid_matrix, piece_mid, piece_mid))

    low = after(jnp.concatenate([low_matrix, low_update], axis=1), forward_mid)
    low = lax.all_gather(low, BLOCK, axis=0, tiled=False)

    lifted = product_rows(gather(forward_mid, BLOCK), mid_update, piece_mid, piece_top)
    share = jnp.where(half == mid_pos, rhs_pair.astype(F32)[None], 0.0)
    share = (share.reshape(SMALL) - lifted).astype(BF16)
    right_top = rounded(mask_top, share.astype(F32) + swap(share, "mid").astype(F32))

    columns = gather(right_top, BLOCK)
    forward_top = rounded(mask_top, product_rows(columns, top_matrix, piece_top, piece_top))
    kept = jnp.concatenate([forward_mid, forward_low], axis=0)
    sent = root_transposed(table, gather(forward_top, FRONT), top_matrix, kept, piece_top)
    solution_top, forward_mid, forward_low, sent = root_collect(
        table, 0, exchange(sent, BLOCK), piece_top
    )
    sent = backward_residual(
        table, 1, exchange(sent, FRONT), forward_mid, middle, piece_top, piece_mid
    )
    solution_mid, sent = backward_solve(table, 1, exchange(sent, FRONT), middle, piece_mid)
    sent = backward_residual(
        table, 2, exchange(sent, FRONT), forward_low, low, piece_mid, piece_low
    )
    solution_low, _ = backward_solve(table, 2, exchange(sent, FRONT), low, piece_low)

    own_mid = lax.dynamic_slice_in_dim(solution_mid, low_pos * piece_mid, piece_mid, 0)
    own_top = lax.dynamic_slice_in_dim(
        solution_top, (mid_pos * 2 + low_pos) * piece_top, piece_top, 0
    )
    solved = from_slices(jnp.concatenate([solution_low, own_mid, own_top], axis=0))
    solution_low = solved[:piece_low]
    solution_mid = solved[piece_low : piece_low + piece_mid]
    solution_top = solved[piece_low + piece_mid :]

    moved = lax.dot_general(
        coupling, solution_low, (((0,), (0,)), ((), ())), preferred_element_type=F32
    )
    shifted = (below_solved.astype(F32) - moved).astype(BF16)
    solution_sub = lax.dot_general(
        subtree_inverse, shifted, (((0,), (0,)), ((), ())), preferred_element_type=F32
    ).astype(BF16)
    return (solution_sub, solution_top, solution_mid, solution_low)


def solution(mesh):
    fine = Mesh(mesh.devices.reshape(2, 2, 4, 2, 4, 4), LEAF + FRONT)
    rows = P(LEAF + FRONT, None)
    placed = (rows,) * 6 + (
        P(None, FRONT, None, LEAF),
        P(None, FRONT, None, LEAF),
        P(None, FRONT, None, LEAF),
        P(None, FRONT, None, None, LEAF),
        P(None, FRONT, None, None, LEAF),
        P(),
    )
    return jax.shard_map(
        shards, mesh=fine, in_specs=placed, out_specs=(rows, rows, rows, rows), check_vma=False
    )
```

```python
import jax
import jax.numpy as jnp
from jax import lax
from jax.experimental import pallas as pl
from jax.experimental.pallas import tpu as pltpu
from jax.sharding import Mesh, PartitionSpec as P

FRONT = ("x", "y")
LEAF = ("mid", "low", "z", "core")
BLOCK = ("z", "core")
WAYS = 16
MEMBERS = 8
SLICE = 32
ROWS = 32
WIDTH = MEMBERS * SLICE
SMALL = (ROWS, WIDTH)
SENT = (WAYS, ROWS, WIDTH)
FRONT_AT, MID_AT, CORE_AT, LOW_AT = 3, 4, 5, 6
F32 = jnp.float32
BF16 = jnp.bfloat16


def swap(array, axis):
    return lax.ppermute(array, axis, [(0, 1), (1, 0)])


def exchange(blocks, axes):
    return lax.all_to_all(blocks, axes, 0, 0, tiled=True)


def gather(block, axes):
    ways = lax.axis_size(axes)
    return exchange(jnp.broadcast_to(block[None], (ways,) + block.shape), axes)


def in_order(position, own, other, axis):
    return jnp.where(
        position == 0,
        jnp.concatenate([own, other], axis=axis),
        jnp.concatenate([other, own], axis=axis),
    )


def product_rows(gathered, matrix, piece, out_piece):
    columns = gathered.reshape(MEMBERS, ROWS // piece, piece, WIDTH)
    columns = columns.transpose(1, 0, 2, 3).reshape(MEMBERS * ROWS, WIDTH)
    product = lax.dot_general(
        matrix, columns, (((0,), (0,)), ((), ())), preferred_element_type=F32
    ).astype(BF16)
    product = product.reshape(ROWS // out_piece, WAYS, out_piece, WIDTH).transpose(1, 0, 2, 3)
    return jnp.sum(exchange(product.reshape(SENT), FRONT).astype(F32), axis=0)


def lane_group(rows):
    return lax.broadcasted_iota(jnp.int32, (rows, WIDTH), 1) // SLICE


def packed_mask(table_ref, level, piece):
    row = lax.broadcasted_iota(jnp.int32, SMALL, 0)
    member = row // piece * MEMBERS + lane_group(ROWS)
    index = (member * WAYS + table_ref[FRONT_AT]) * piece + row % piece
    return index < table_ref[level]


def source_rows(recv_ref, piece):
    parts = []
    for o in range(ROWS // piece):
        rows = recv_ref[:, o * piece : (o + 1) * piece, :].astype(F32)
        parts.append(rows.reshape(WAYS * piece, WIDTH))
    return jnp.concatenate(parts, axis=0).astype(BF16)


def apply_transposed(weights_ref, recv_ref, row_piece, piece):
    source = source_rows(recv_ref, row_piece)
    group = lane_group(WIDTH)
    total = jnp.zeros((WIDTH, WIDTH), F32)
    for m in range(MEMBERS):
        term = jnp.dot(weights_ref[m], source, preferred_element_type=F32)
        total = jnp.where(group == m, term, total)
    for step in (4 * SLICE, 2 * SLICE, SLICE):
        total = total + pltpu.roll(total, step, 1)
    group = lane_group(piece)
    packed = []
    for o in range(ROWS // piece):
        rows = jnp.zeros((piece, WIDTH), F32)
        for m in range(MEMBERS):
            start = (o * MEMBERS + m) * piece
            rows = jnp.where(group == m, total[start : start + piece], rows)
        packed.append(rows)
    return jnp.concatenate(packed, axis=0)


def whole(shape):
    return pl.BlockSpec(shape, lambda i: (0,) * len(shape))


def call(body, table, operands, specs, shapes):
    return pl.pallas_call(
        body,
        grid=(1,),
        in_specs=[pl.BlockSpec(memory_space=pltpu.SMEM)] + specs,
        out_specs=[whole(shape) for shape in shapes],
        out_shape=[jax.ShapeDtypeStruct(shape, BF16) for shape in shapes],
        compiler_params=pltpu.CompilerParams(vmem_limit_bytes=32 << 20),
    )(table, *operands)


def weight_spec(part):
    return pl.BlockSpec((MEMBERS, WIDTH, 2 * WIDTH), lambda i: (0, 0, part))


READY = (8, 128)


def backward_solve(table, level, recv, weights, piece, ready):
    def body(table_ref, recv_ref, weights_ref, ready_ref, solved_ref, send_ref):
        value = apply_transposed(weights_ref, recv_ref, piece, piece)
        solved = jnp.where(packed_mask(table_ref, level, piece), value, 0.0).astype(BF16)
        solved_ref[...] = solved
        send_ref[...] = jnp.broadcast_to(solved[None], SENT)

    return call(
        body,
        table,
        (recv, weights, ready),
        [whole(SENT), weight_spec(0), whole(READY)],
        [SMALL, SENT],
    )


def backward_residual(table, level, recv, forward, weights, row_piece, piece):
    def body(table_ref, recv_ref, forward_ref, weights_ref, send_ref):
        value = forward_ref[...].astype(F32)
        value = value - apply_transposed(weights_ref, recv_ref, row_piece, piece)
        residual = jnp.where(packed_mask(table_ref, level, piece), value, 0.0).astype(BF16)
        send_ref[...] = jnp.broadcast_to(residual[None], SENT)

    return call(
        body,
        table,
        (recv, forward, weights),
        [whole(SENT), whole(SMALL), weight_spec(1)],
        [SENT],
    )[0]


def order_shares(table, shares, low_matrix, low_update, chain):
    def body(
        table_ref,
        shares_ref,
        low_matrix_ref,
        low_update_ref,
        chain_ref,
        middle_ref,
        matrix_ref,
        update_ref,
        root_ref,
        low_ref,
    ):
        low_ref[:, : 2 * WIDTH] = low_matrix_ref[...]
        low_ref[:, 2 * WIDTH :] = low_update_ref[...]
        core = table_ref[CORE_AT]
        for o in range(2):
            block = shares_ref[table_ref[MID_AT] * 4 + o * 2 + core, :, :WIDTH]
            matrix_ref[:, o * WIDTH : (o + 1) * WIDTH] = block
            middle_ref[:, o * WIDTH : (o + 1) * WIDTH] = block
            for h in range(2):
                block = shares_ref[table_ref[MID_AT] * 4 + o * 2 + core, :, WIDTH + h * 128 : WIDTH + h * 128 + 128]
                start = (h * 2 + o) * 128
                update_ref[:, start : start + 128] = block
                middle_ref[:, 2 * WIDTH + start : 2 * WIDTH + start + 128] = block
        for o in range(4):
            root_ref[:, o * 128 : o * 128 + 128] = shares_ref[o * 2 + core, :, 2 * WIDTH :]

    pair = (WIDTH, 2 * WIDTH)
    return call(
        body,
        table,
        (shares, low_matrix, low_update, chain),
        [whole(shares.shape), whole(pair), whole(pair), pl.BlockSpec(memory_space=pl.ANY)],
        [(WIDTH, 4 * WIDTH), pair, pair, pair, (WIDTH, 4 * WIDTH)],
    )


def cut_rows(rows, group):
    turned = [rows] + [pltpu.roll(rows, SLICE * d, 1) for d in range(1, MEMBERS)]
    pieces = []
    for target in range(MEMBERS):
        piece = jnp.zeros((8, WIDTH), F32)
        for q in range(8):
            piece = jnp.where(group == q, turned[(q - target) % MEMBERS][q * 8 : q * 8 + 8], piece)
        pieces.append(piece)
    return pieces


def join_rows(pieces, group, count):
    joined = []
    for q in range(count):
        rows = jnp.zeros((8, WIDTH), F32)
        for m in range(MEMBERS):
            shift = (m - q) % MEMBERS
            moved = pltpu.roll(pieces[m], SLICE * shift, 1) if shift else pieces[m]
            rows = jnp.where(group == m, moved, rows)
        joined.append(rows)
    return joined


def final_solve(table, level, recv, weights, piece, solved_mid, solved_top):
    def body(table_ref, recv_ref, weights_ref, mid_ref, top_ref, send_ref):
        value = apply_transposed(weights_ref, recv_ref, piece, piece)
        solved = jnp.where(packed_mask(table_ref, level, piece), value, 0.0)
        mid_rows = mid_ref[...].astype(F32)
        mid_rows = jnp.where(table_ref[LOW_AT] == 0, mid_rows[:16], mid_rows[16:])
        top_rows = top_ref[...].astype(F32)
        own = table_ref[MID_AT] * 2 + table_ref[LOW_AT]
        own_top = top_rows[:8]
        for o in range(1, 4):
            own_top = jnp.where(own == o, top_rows[o * 8 : o * 8 + 8], own_top)
        rows = jnp.concatenate([solved, mid_rows, own_top, jnp.zeros((8, WIDTH), F32)], axis=0)
        for target, cut in enumerate(cut_rows(rows, lane_group(8))):
            send_ref[target] = cut.astype(BF16)

    return call(
        body,
        table,
        (recv, weights, solved_mid, solved_top),
        [whole(SENT), weight_spec(0), whole(SMALL), whole(SMALL)],
        [(MEMBERS, 8, WIDTH)],
    )[0]


def final_rows(table, recv):
    def body(table_ref, recv_ref, low_ref, mid_ref, top_ref):
        pieces = [recv_ref[m].astype(F32) for m in range(MEMBERS)]
        rows = join_rows(pieces, lane_group(8), 7)
        low_ref[...] = jnp.concatenate(rows[:4], axis=0).astype(BF16)
        mid_ref[...] = jnp.concatenate(rows[4:6], axis=0).astype(BF16)
        top_ref[...] = rows[6].astype(BF16)

    shapes = [SMALL, (16, WIDTH), (8, WIDTH)]
    return call(body, table, (recv,), [whole((MEMBERS, 8, WIDTH))], shapes)


SPLIT = (MEMBERS, ROWS + 8, WIDTH)


def root_transposed(table, recv, matrix, kept, piece, ready):
    def body(table_ref, recv_ref, matrix_ref, kept_ref, ready_ref, send_ref):
        product = jnp.dot(
            matrix_ref[...], source_rows(recv_ref, piece), preferred_element_type=F32
        )
        kept_rows = kept_ref[...].astype(F32)
        turned = [product] + [pltpu.roll(product, SLICE * d, 1) for d in range(1, MEMBERS)]
        group = lane_group(8)
        cut = cut_rows(kept_rows, group)
        for target in range(MEMBERS):
            blocks = []
            for o in range(ROWS // piece):
                rows = jnp.zeros((piece, WIDTH), F32)
                for m in range(MEMBERS):
                    start = (o * MEMBERS + m) * piece
                    moved = turned[(m - target) % MEMBERS][start : start + piece]
                    rows = jnp.where(group == m, moved, rows)
                blocks.append(rows)
            blocks.append(cut[target])
            send_ref[target] = jnp.concatenate(blocks, axis=0).astype(BF16)

    return call(
        body,
        table,
        (recv, matrix, kept, ready),
        [whole(SENT), whole((WIDTH, 2 * WIDTH)), whole((2 * ROWS, WIDTH)), whole(READY)],
        [SPLIT],
    )[0]


def root_collect(table, level, recv, piece):
    def body(table_ref, recv_ref, solved_ref, mid_ref, low_ref, send_ref):
        blocks = [recv_ref[m].astype(F32) for m in range(MEMBERS)]
        total = blocks[0][:ROWS]
        for m in range(1, MEMBERS):
            total = total + blocks[m][:ROWS]
        solved = jnp.where(packed_mask(table_ref, level, piece), total, 0.0).astype(BF16)
        solved_ref[...] = solved
        send_ref[...] = jnp.broadcast_to(solved[None], SENT)
        pieces = [block[ROWS:] for block in blocks]
        kept = join_rows(pieces, lane_group(8), 8)
        mid_ref[...] = jnp.concatenate(kept[:4], axis=0).astype(BF16)
        low_ref[...] = jnp.concatenate(kept[4:], axis=0).astype(BF16)

    return call(body, table, (recv,), [whole(SPLIT)], [SMALL, SMALL, SMALL, SENT])


def shards(
    subtree_rhs,
    subtree_inverse,
    coupling,
    rhs_top,
    rhs_mid,
    rhs_low,
    inverse_top,
    inverse_mid,
    inverse_low,
    update_mid,
    update_low,
    front_rows,
):
    mid_pos = lax.axis_index("mid")
    low_pos = lax.axis_index("low")
    front_pos = lax.axis_index(FRONT)
    member = lax.axis_index(BLOCK)
    piece_top, piece_mid, piece_low = rhs_top.shape[0], rhs_mid.shape[0], rhs_low.shape[0]
    low_matrix = inverse_low.reshape(WIDTH, -1)
    low_update = update_low.reshape(WIDTH, -1)

    lookup = jnp.arange(front_rows.shape[0], dtype=jnp.int32)

    def live(index):
        return jnp.sum(jnp.where(lookup == index, front_rows, 0))

    def row_mask(live_rows, piece):
        row = jnp.arange(ROWS, dtype=jnp.int32)
        place = (row // piece * MEMBERS + member) * WAYS + front_pos
        return (place * piece + row % piece < live_rows)[:, None]

    live_top, live_mid, live_low = live(0), live(1 + mid_pos), live(3 + mid_pos * 2 + low_pos)
    table = jnp.stack(
        [live_top, live_mid, live_low, front_pos, mid_pos, lax.axis_index("core"), low_pos]
    ).astype(jnp.int32)
    mask_top = row_mask(live_top, piece_top)
    mask_mid = row_mask(live_mid, piece_mid)
    mask_low = row_mask(live_low, piece_low)

    def rounded(mask, value):
        return jnp.where(mask, value, 0.0).astype(BF16)

    below_solved = jnp.dot(subtree_inverse, subtree_rhs, preferred_element_type=F32).astype(BF16)
    pushed = jnp.dot(coupling, below_solved, preferred_element_type=F32)
    right_low = rounded(mask_low, rhs_low.astype(F32) - pushed)
    columns = gather(right_low, BLOCK)
    own = jnp.concatenate(
        [
            inverse_mid.reshape(WIDTH, -1),
            update_mid.reshape(WIDTH, -1),
            inverse_top.reshape(WIDTH, -1),
        ],
        axis=1,
    )
    shares = lax.all_gather(own, ("mid", "low", "core"), axis=0, tiled=False)
    forward_low = rounded(mask_low, product_rows(columns, low_matrix, piece_low, piece_low))

    lifted = product_rows(gather(forward_low, BLOCK), low_update, piece_low, piece_mid)
    half = jnp.arange(2, dtype=jnp.int32)[:, None, None]
    share = jnp.where(half == low_pos, rhs_mid.astype(F32)[None], 0.0)
    share = (share.reshape(SMALL) - lifted).astype(BF16)
    shared = swap(jnp.concatenate([share, rhs_top], axis=0), "low")
    right_mid = rounded(mask_mid, share.astype(F32) + shared[:ROWS].astype(F32))
    rhs_pair = in_order(low_pos, rhs_top, shared[ROWS:], 0)

    columns = gather(right_mid, BLOCK)
    middle, mid_matrix, mid_update, top_matrix, low = order_shares(
        table, shares, low_matrix, low_update, right_mid
    )
    middle = lax.all_gather(middle, BLOCK, axis=0, tiled=False)
    forward_mid = rounded(mask_mid, product_rows(columns, mid_matrix, piece_mid, piece_mid))

    low = lax.all_gather(low, BLOCK, axis=0, tiled=False)

    lifted = product_rows(gather(forward_mid, BLOCK), mid_update, piece_mid, piece_top)
    share = jnp.where(half == mid_pos, rhs_pair.astype(F32)[None], 0.0)
    share = (share.reshape(SMALL) - lifted).astype(BF16)
    right_top = rounded(mask_top, share.astype(F32) + swap(share, "mid").astype(F32))

    columns = gather(right_top, BLOCK)
    forward_top = rounded(mask_top, product_rows(columns, top_matrix, piece_top, piece_top))
    kept = jnp.concatenate([forward_mid, forward_low], axis=0)
    sent = root_transposed(
        table, gather(forward_top, FRONT), top_matrix, kept, piece_top, middle[0, :8, :128]
    )
    solution_top, forward_mid, forward_low, sent = root_collect(
        table, 0, exchange(sent, BLOCK), piece_top
    )
    sent = backward_residual(
        table, 1, exchange(sent, FRONT), forward_mid, middle, piece_top, piece_mid
    )
    solution_mid, sent = backward_solve(
        table, 1, exchange(sent, FRONT), middle, piece_mid, low[0, :8, :128]
    )
    sent = backward_residual(
        table, 2, exchange(sent, FRONT), forward_low, low, piece_mid, piece_low
    )
    sent = final_solve(
        table, 2, exchange(sent, FRONT), low, piece_low, solution_mid, solution_top
    )
    solution_low, solution_mid, solution_top = final_rows(table, exchange(sent, BLOCK))

    moved = lax.dot_general(
        coupling, solution_low, (((0,), (0,)), ((), ())), preferred_element_type=F32
    )
    shifted = (below_solved.astype(F32) - moved).astype(BF16)
    solution_sub = lax.dot_general(
        subtree_inverse, shifted, (((0,), (0,)), ((), ())), preferred_element_type=F32
    ).astype(BF16)
    return (solution_sub, solution_top, solution_mid, solution_low)


def solution(mesh):
    fine = Mesh(mesh.devices.reshape(2, 2, 4, 2, 4, 4), LEAF + FRONT)
    rows = P(LEAF + FRONT, None)
    placed = (rows,) * 6 + (
        P(None, FRONT, None, LEAF),
        P(None, FRONT, None, LEAF),
        P(None, FRONT, None, LEAF),
        P(None, FRONT, None, None, LEAF),
        P(None, FRONT, None, None, LEAF),
        P(),
    )
    return jax.shard_map(
        shards, mesh=fine, in_specs=placed, out_specs=(rows, rows, rows, rows), check_vma=False
    )
```

```python
import jax
import jax.numpy as jnp
from jax import lax
from jax.experimental import pallas as pl
from jax.experimental.pallas import tpu as pltpu
from jax.sharding import Mesh, PartitionSpec as P

FRONT = ("x", "y")
LEAF = ("mid", "low", "z", "core")
BLOCK = ("z", "core")
WAYS = 16
MEMBERS = 8
SLICE = 32
ROWS = 32
WIDTH = MEMBERS * SLICE
SMALL = (ROWS, WIDTH)
SENT = (WAYS, ROWS, WIDTH)
FRONT_AT, MID_AT, CORE_AT, LOW_AT = 3, 4, 5, 6
F32 = jnp.float32
BF16 = jnp.bfloat16


def swap(array, axis):
    return lax.ppermute(array, axis, [(0, 1), (1, 0)])


def exchange(blocks, axes):
    return lax.all_to_all(blocks, axes, 0, 0, tiled=True)


def gather(block, axes):
    ways = lax.axis_size(axes)
    return exchange(jnp.broadcast_to(block[None], (ways,) + block.shape), axes)


def in_order(position, own, other, axis):
    return jnp.where(
        position == 0,
        jnp.concatenate([own, other], axis=axis),
        jnp.concatenate([other, own], axis=axis),
    )


def product_rows(gathered, matrix, piece, out_piece):
    columns = gathered.reshape(MEMBERS, ROWS // piece, piece, WIDTH)
    columns = columns.transpose(1, 0, 2, 3).reshape(MEMBERS * ROWS, WIDTH)
    product = lax.dot_general(
        matrix, columns, (((0,), (0,)), ((), ())), preferred_element_type=F32
    ).astype(BF16)
    product = product.reshape(ROWS // out_piece, WAYS, out_piece, WIDTH).transpose(1, 0, 2, 3)
    return jnp.sum(exchange(product.reshape(SENT), FRONT).astype(F32), axis=0)


def lane_group(rows):
    return lax.broadcasted_iota(jnp.int32, (rows, WIDTH), 1) // SLICE


def packed_mask(table_ref, level, piece):
    row = lax.broadcasted_iota(jnp.int32, SMALL, 0)
    member = row // piece * MEMBERS + lane_group(ROWS)
    index = (member * WAYS + table_ref[FRONT_AT]) * piece + row % piece
    return index < table_ref[level]


def source_rows(recv_ref, piece):
    parts = []
    for o in range(ROWS // piece):
        rows = recv_ref[:, o * piece : (o + 1) * piece, :].astype(F32)
        parts.append(rows.reshape(WAYS * piece, WIDTH))
    return jnp.concatenate(parts, axis=0).astype(BF16)


def apply_transposed(weights_ref, recv_ref, row_piece, piece):
    source = source_rows(recv_ref, row_piece)
    group = lane_group(WIDTH)
    total = jnp.zeros((WIDTH, WIDTH), F32)
    for m in range(MEMBERS):
        term = jnp.dot(weights_ref[m], source, preferred_element_type=F32)
        total = jnp.where(group == m, term, total)
    for step in (4 * SLICE, 2 * SLICE, SLICE):
        total = total + pltpu.roll(total, step, 1)
    group = lane_group(piece)
    packed = []
    for o in range(ROWS // piece):
        rows = jnp.zeros((piece, WIDTH), F32)
        for m in range(MEMBERS):
            start = (o * MEMBERS + m) * piece
            rows = jnp.where(group == m, total[start : start + piece], rows)
        packed.append(rows)
    return jnp.concatenate(packed, axis=0)


def whole(shape):
    return pl.BlockSpec(shape, lambda i: (0,) * len(shape))


def call(body, table, operands, specs, shapes):
    return pl.pallas_call(
        body,
        grid=(1,),
        in_specs=[pl.BlockSpec(memory_space=pltpu.SMEM)] + specs,
        out_specs=[whole(shape) for shape in shapes],
        out_shape=[jax.ShapeDtypeStruct(shape, BF16) for shape in shapes],
        compiler_params=pltpu.CompilerParams(vmem_limit_bytes=32 << 20),
    )(table, *operands)


def weight_spec(part):
    return pl.BlockSpec((MEMBERS, WIDTH, 2 * WIDTH), lambda i: (0, 0, part))


READY = (8, 128)


def backward_solve(table, level, recv, weights, piece, ready):
    def body(table_ref, recv_ref, weights_ref, ready_ref, solved_ref, send_ref):
        value = apply_transposed(weights_ref, recv_ref, piece, piece)
        solved = jnp.where(packed_mask(table_ref, level, piece), value, 0.0).astype(BF16)
        solved_ref[...] = solved
        send_ref[...] = jnp.broadcast_to(solved[None], SENT)

    return call(
        body,
        table,
        (recv, weights, ready),
        [whole(SENT), weight_spec(0), whole(READY)],
        [SMALL, SENT],
    )


def backward_residual(table, level, recv, forward, weights, part, row_piece, piece):
    def body(table_ref, recv_ref, forward_ref, weights_ref, send_ref):
        value = forward_ref[...].astype(F32)
        value = value - apply_transposed(weights_ref, recv_ref, row_piece, piece)
        residual = jnp.where(packed_mask(table_ref, level, piece), value, 0.0).astype(BF16)
        send_ref[...] = jnp.broadcast_to(residual[None], SENT)

    return call(
        body,
        table,
        (recv, forward, weights),
        [whole(SENT), whole(SMALL), weight_spec(part)],
        [SENT],
    )[0]


def order_shares(table, shares, low_matrix, low_update, chain):
    def body(
        table_ref,
        shares_ref,
        low_matrix_ref,
        low_update_ref,
        chain_ref,
        matrix_ref,
        update_ref,
        root_ref,
        low_ref,
    ):
        low_ref[:, : 2 * WIDTH] = low_matrix_ref[...]
        low_ref[:, 2 * WIDTH :] = low_update_ref[...]
        core = table_ref[CORE_AT]
        for o in range(2):
            block = shares_ref[table_ref[MID_AT] * 4 + o * 2 + core, :, :WIDTH]
            matrix_ref[:, o * WIDTH : (o + 1) * WIDTH] = block
            for h in range(2):
                block = shares_ref[table_ref[MID_AT] * 4 + o * 2 + core, :, WIDTH + h * 128 : WIDTH + h * 128 + 128]
                start = (h * 2 + o) * 128
                update_ref[:, start : start + 128] = block
        for o in range(4):
            root_ref[:, o * 128 : o * 128 + 128] = shares_ref[o * 2 + core, :, 2 * WIDTH :]

    pair = (WIDTH, 2 * WIDTH)
    return call(
        body,
        table,
        (shares, low_matrix, low_update, chain),
        [whole(shares.shape), whole(pair), whole(pair), pl.BlockSpec(memory_space=pl.ANY)],
        [pair, pair, pair, (WIDTH, 4 * WIDTH)],
    )


def cut_rows(rows, group):
    turned = [rows] + [pltpu.roll(rows, SLICE * d, 1) for d in range(1, MEMBERS)]
    pieces = []
    for target in range(MEMBERS):
        piece = jnp.zeros((8, WIDTH), F32)
        for q in range(8):
            piece = jnp.where(group == q, turned[(q - target) % MEMBERS][q * 8 : q * 8 + 8], piece)
        pieces.append(piece)
    return pieces


def join_rows(pieces, group, count):
    joined = []
    for q in range(count):
        rows = jnp.zeros((8, WIDTH), F32)
        for m in range(MEMBERS):
            shift = (m - q) % MEMBERS
            moved = pltpu.roll(pieces[m], SLICE * shift, 1) if shift else pieces[m]
            rows = jnp.where(group == m, moved, rows)
        joined.append(rows)
    return joined


def final_solve(table, level, recv, weights, piece, solved_mid, solved_top):
    def body(table_ref, recv_ref, weights_ref, mid_ref, top_ref, send_ref):
        value = apply_transposed(weights_ref, recv_ref, piece, piece)
        solved = jnp.where(packed_mask(table_ref, level, piece), value, 0.0)
        mid_rows = mid_ref[...].astype(F32)
        mid_rows = jnp.where(table_ref[LOW_AT] == 0, mid_rows[:16], mid_rows[16:])
        top_rows = top_ref[...].astype(F32)
        own = table_ref[MID_AT] * 2 + table_ref[LOW_AT]
        own_top = top_rows[:8]
        for o in range(1, 4):
            own_top = jnp.where(own == o, top_rows[o * 8 : o * 8 + 8], own_top)
        rows = jnp.concatenate([solved, mid_rows, own_top, jnp.zeros((8, WIDTH), F32)], axis=0)
        for target, cut in enumerate(cut_rows(rows, lane_group(8))):
            send_ref[target] = cut.astype(BF16)

    return call(
        body,
        table,
        (recv, weights, solved_mid, solved_top),
        [whole(SENT), weight_spec(0), whole(SMALL), whole(SMALL)],
        [(MEMBERS, 8, WIDTH)],
    )[0]


def final_rows(table, recv):
    def body(table_ref, recv_ref, low_ref, mid_ref, top_ref):
        pieces = [recv_ref[m].astype(F32) for m in range(MEMBERS)]
        rows = join_rows(pieces, lane_group(8), 7)
        low_ref[...] = jnp.concatenate(rows[:4], axis=0).astype(BF16)
        mid_ref[...] = jnp.concatenate(rows[4:6], axis=0).astype(BF16)
        top_ref[...] = rows[6].astype(BF16)

    shapes = [SMALL, (16, WIDTH), (8, WIDTH)]
    return call(body, table, (recv,), [whole((MEMBERS, 8, WIDTH))], shapes)


SPLIT = (MEMBERS, ROWS + 8, WIDTH)


def root_transposed(table, recv, matrix, kept, piece, ready):
    def body(table_ref, recv_ref, matrix_ref, kept_ref, ready_ref, send_ref):
        product = jnp.dot(
            matrix_ref[...], source_rows(recv_ref, piece), preferred_element_type=F32
        )
        kept_rows = kept_ref[...].astype(F32)
        turned = [product] + [pltpu.roll(product, SLICE * d, 1) for d in range(1, MEMBERS)]
        group = lane_group(8)
        cut = cut_rows(kept_rows, group)
        for target in range(MEMBERS):
            blocks = []
            for o in range(ROWS // piece):
                rows = jnp.zeros((piece, WIDTH), F32)
                for m in range(MEMBERS):
                    start = (o * MEMBERS + m) * piece
                    moved = turned[(m - target) % MEMBERS][start : start + piece]
                    rows = jnp.where(group == m, moved, rows)
                blocks.append(rows)
            blocks.append(cut[target])
            send_ref[target] = jnp.concatenate(blocks, axis=0).astype(BF16)

    return call(
        body,
        table,
        (recv, matrix, kept, ready),
        [whole(SENT), whole((WIDTH, 2 * WIDTH)), whole((2 * ROWS, WIDTH)), whole(READY)],
        [SPLIT],
    )[0]


def root_collect(table, level, recv, piece):
    def body(table_ref, recv_ref, solved_ref, mid_ref, low_ref, send_ref):
        blocks = [recv_ref[m].astype(F32) for m in range(MEMBERS)]
        total = blocks[0][:ROWS]
        for m in range(1, MEMBERS):
            total = total + blocks[m][:ROWS]
        solved = jnp.where(packed_mask(table_ref, level, piece), total, 0.0).astype(BF16)
        solved_ref[...] = solved
        send_ref[...] = jnp.broadcast_to(solved[None], SENT)
        pieces = [block[ROWS:] for block in blocks]
        kept = join_rows(pieces, lane_group(8), 8)
        mid_ref[...] = jnp.concatenate(kept[:4], axis=0).astype(BF16)
        low_ref[...] = jnp.concatenate(kept[4:], axis=0).astype(BF16)

    return call(body, table, (recv,), [whole(SPLIT)], [SMALL, SMALL, SMALL, SENT])


def shards(
    subtree_rhs,
    subtree_inverse,
    coupling,
    rhs_top,
    rhs_mid,
    rhs_low,
    inverse_top,
    inverse_mid,
    inverse_low,
    update_mid,
    update_low,
    front_rows,
):
    mid_pos = lax.axis_index("mid")
    low_pos = lax.axis_index("low")
    front_pos = lax.axis_index(FRONT)
    member = lax.axis_index(BLOCK)
    piece_top, piece_mid, piece_low = rhs_top.shape[0], rhs_mid.shape[0], rhs_low.shape[0]
    low_matrix = inverse_low.reshape(WIDTH, -1)
    low_update = update_low.reshape(WIDTH, -1)

    lookup = jnp.arange(front_rows.shape[0], dtype=jnp.int32)

    def live(index):
        return jnp.sum(jnp.where(lookup == index, front_rows, 0))

    def row_mask(live_rows, piece):
        row = jnp.arange(ROWS, dtype=jnp.int32)
        place = (row // piece * MEMBERS + member) * WAYS + front_pos
        return (place * piece + row % piece < live_rows)[:, None]

    live_top, live_mid, live_low = live(0), live(1 + mid_pos), live(3 + mid_pos * 2 + low_pos)
    table = jnp.stack(
        [live_top, live_mid, live_low, front_pos, mid_pos, lax.axis_index("core"), low_pos]
    ).astype(jnp.int32)
    mask_top = row_mask(live_top, piece_top)
    mask_mid = row_mask(live_mid, piece_mid)
    mask_low = row_mask(live_low, piece_low)

    def rounded(mask, value):
        return jnp.where(mask, value, 0.0).astype(BF16)

    below_solved = jnp.dot(subtree_inverse, subtree_rhs, preferred_element_type=F32).astype(BF16)
    pushed = jnp.dot(coupling, below_solved, preferred_element_type=F32)
    right_low = rounded(mask_low, rhs_low.astype(F32) - pushed)
    columns = gather(right_low, BLOCK)
    own = jnp.concatenate(
        [
            inverse_mid.reshape(WIDTH, -1),
            update_mid.reshape(WIDTH, -1),
            inverse_top.reshape(WIDTH, -1),
        ],
        axis=1,
    )
    shares = lax.all_gather(own, ("mid", "low", "core"), axis=0, tiled=False)
    forward_low = rounded(mask_low, product_rows(columns, low_matrix, piece_low, piece_low))

    lifted = product_rows(gather(forward_low, BLOCK), low_update, piece_low, piece_mid)
    half = jnp.arange(2, dtype=jnp.int32)[:, None, None]
    share = jnp.where(half == low_pos, rhs_mid.astype(F32)[None], 0.0)
    share = (share.reshape(SMALL) - lifted).astype(BF16)
    shared = swap(jnp.concatenate([share, rhs_top], axis=0), "low")
    right_mid = rounded(mask_mid, share.astype(F32) + shared[:ROWS].astype(F32))
    rhs_pair = in_order(low_pos, rhs_top, shared[ROWS:], 0)

    columns = gather(right_mid, BLOCK)
    mid_matrix, mid_update, top_matrix, low = order_shares(
        table, shares, low_matrix, low_update, right_mid
    )
    all_update = lax.all_gather(mid_update, BLOCK, axis=0, tiled=False)
    all_matrix = lax.all_gather(mid_matrix, BLOCK, axis=0, tiled=False)
    forward_mid = rounded(mask_mid, product_rows(columns, mid_matrix, piece_mid, piece_mid))

    low = lax.all_gather(low, BLOCK, axis=0, tiled=False)

    lifted = product_rows(gather(forward_mid, BLOCK), mid_update, piece_mid, piece_top)
    share = jnp.where(half == mid_pos, rhs_pair.astype(F32)[None], 0.0)
    share = (share.reshape(SMALL) - lifted).astype(BF16)
    right_top = rounded(mask_top, share.astype(F32) + swap(share, "mid").astype(F32))

    columns = gather(right_top, BLOCK)
    forward_top = rounded(mask_top, product_rows(columns, top_matrix, piece_top, piece_top))
    kept = jnp.concatenate([forward_mid, forward_low], axis=0)
    sent = root_transposed(
        table, gather(forward_top, FRONT), top_matrix, kept, piece_top, all_update[0, :8, :128]
    )
    solution_top, forward_mid, forward_low, sent = root_collect(
        table, 0, exchange(sent, BLOCK), piece_top
    )
    sent = backward_residual(
        table, 1, exchange(sent, FRONT), forward_mid, all_update, 0, piece_top, piece_mid
    )
    solution_mid, sent = backward_solve(
        table, 1, exchange(sent, FRONT), all_matrix, piece_mid, low[0, :8, :128]
    )
    sent = backward_residual(
        table, 2, exchange(sent, FRONT), forward_low, low, 1, piece_mid, piece_low
    )
    sent = final_solve(
        table, 2, exchange(sent, FRONT), low, piece_low, solution_mid, solution_top
    )
    solution_low, solution_mid, solution_top = final_rows(table, exchange(sent, BLOCK))

    moved = lax.dot_general(
        coupling, solution_low, (((0,), (0,)), ((), ())), preferred_element_type=F32
    )
    shifted = (below_solved.astype(F32) - moved).astype(BF16)
    solution_sub = lax.dot_general(
        subtree_inverse, shifted, (((0,), (0,)), ((), ())), preferred_element_type=F32
    ).astype(BF16)
    return (solution_sub, solution_top, solution_mid, solution_low)


def solution(mesh):
    fine = Mesh(mesh.devices.reshape(2, 2, 4, 2, 4, 4), LEAF + FRONT)
    rows = P(LEAF + FRONT, None)
    placed = (rows,) * 6 + (
        P(None, FRONT, None, LEAF),
        P(None, FRONT, None, LEAF),
        P(None, FRONT, None, LEAF),
        P(None, FRONT, None, None, LEAF),
        P(None, FRONT, None, None, LEAF),
        P(),
    )
    return jax.shard_map(
        shards, mesh=fine, in_specs=placed, out_specs=(rows, rows, rows, rows), check_vma=False
    )
```
